32 devices in a mesh: dp: 8 (over z, core), fsdp: 4 (over y, x).
Axes of the slice: x: 2, y: 2, z: 4, core: 2. Of those that a mesh axis runs over, the one named last changes fastest.
Arguments:
- tokens: bfloat16 [32768, 768], P(('dp', 'fsdp')), may hold values from -6 to 6
- latents: bfloat16 [1024, 768], P(('dp', 'fsdp')), may hold values from -6 to 6
- valid_mask: int32 [32768], P(('dp', 'fsdp')), may hold values from 0 to 1, as said below
- out_cotangent: bfloat16 [32768, 768], P(('dp', 'fsdp')), may hold values from -6 to 6
- latent_cotangent: bfloat16 [1024, 768], P(('dp', 'fsdp')), may hold values from -6 to 6
- norm_gains: bfloat16 [8, 768], P(None, ('dp', 'fsdp')), may hold values from 0.5 to 1.5
- local_qkv: bfloat16 [2304, 768], P(('dp', 'fsdp')), may hold values from -0.21875 to 0.21875
- local_out: bfloat16 [768, 768], P(('dp', 'fsdp')), may hold values from -0.875 to 0.875
- token_up: bfloat16 [3072, 768], P(('dp', 'fsdp')), may hold values from -0.21875 to 0.21875
- token_down: bfloat16 [768, 3072], P(('dp', 'fsdp')), may hold values from -0.109375 to 0.109375
- read_qkv: bfloat16 [2304, 768], P(('dp', 'fsdp')), may hold values from -0.21875 to 0.21875
- read_out: bfloat16 [768, 768], P(('dp', 'fsdp')), may hold values from -0.875 to 0.875
- global_qkv: bfloat16 [2304, 768], P(('dp', 'fsdp')), may hold values from -0.21875 to 0.21875
- global_out: bfloat16 [768, 768], P(('dp', 'fsdp')), may hold values from -0.625 to 0.625
- latent_up: bfloat16 [3072, 768], P(('dp', 'fsdp')), may hold values from -0.21875 to 0.21875
- latent_down: bfloat16 [768, 3072], P(('dp', 'fsdp')), may hold values from -0.109375 to 0.109375
- write_qkv: bfloat16 [2304, 768], P(('dp', 'fsdp')), may hold values from -0.21875 to 0.21875
- write_out: bfloat16 [768, 768], P(('dp', 'fsdp')), may hold values from -0.3125 to 0.3125
Outputs:
- out_tokens: bfloat16 [32768, 768], P(('dp', 'fsdp'))
- out_latents: bfloat16 [1024, 768], P(('dp', 'fsdp'))
- grad_tokens: float32 [32768, 768], P(('dp', 'fsdp'))
- grad_latents: float32 [1024, 768], P(('dp', 'fsdp'))
- grad_norm_gains: float32 [8, 768], P(None, ('dp', 'fsdp'))
- grad_local_qkv: float32 [2304, 768], P(('dp', 'fsdp'))
- grad_local_out: float32 [768, 768], P(('dp', 'fsdp'))
- grad_token_up: float32 [3072, 768], P(('dp', 'fsdp'))
- grad_token_down: float32 [768, 3072], P(('dp', 'fsdp'))
- grad_read_qkv: float32 [2304, 768], P(('dp', 'fsdp'))
- grad_read_out: float32 [768, 768], P(('dp', 'fsdp'))
- grad_global_qkv: float32 [2304, 768], P(('dp', 'fsdp'))
- grad_global_out: float32 [768, 768], P(('dp', 'fsdp'))
- grad_latent_up: float32 [3072, 768], P(('dp', 'fsdp'))
- grad_latent_down: float32 [768, 3072], P(('dp', 'fsdp'))
- grad_write_qkv: float32 [2304, 768], P(('dp', 'fsdp'))
- grad_write_out: float32 [768, 768], P(('dp', 'fsdp'))
The draws below stay inside these ranges and needn't reach their ends.
Inputs may be any that keep to these rules, and one draw needn't show every extreme that they name: `valid_mask`: within each image of 4096 consecutive slots the valid slots come first and number at least 3841, so every group holds a valid slot.
All inputs are finite; a program needn't handle non-finite values.
Results may differ from the reference program's by a relative error of at most 0.02.
Values may be sent and summed in bfloat16 or wider, within the bound.
A program may use at most 320 MiB of HBM per device.

```python
import jax
import jax.numpy as jnp
from jax import lax

D = 768
HDIM = 64
FF = 3072
GROUP = 256
LAT = 8
SLOTS = 4096
TOKENS = 32768
LATS = 1024


def draw_valid_mask(key, part):
    images = TOKENS // SLOTS
    short_key = jax.random.fold_in(key, 11)
    order_key = jax.random.fold_in(key, 23)
    shortage = jax.random.randint(short_key, (images,), 0, GROUP)
    order = jax.random.permutation(order_key, images)
    shortage = shortage.at[order[0]].set(GROUP - 1)
    shortage = shortage.at[order[1]].set(0)
    counts = SLOTS - shortage
    places = jnp.arange(SLOTS, dtype=jnp.int32)
    return (places[None, :] < counts[:, None]).astype(jnp.int32).reshape(TOKENS)


def block_scale(own_key, shape, cuts, least, high):
    gain, own = 1.0, jax.random.fold_in(own_key, 6)
    for dim, blocks in cuts:
        draws = jnp.exp(jax.random.uniform(jax.random.fold_in(own, dim), (blocks,), jnp.float32, least / len(cuts), high / len(cuts)))
        gain = gain * jnp.repeat(draws, shape[dim] // blocks).reshape([-1 if axis == dim else 1 for axis in range(len(shape))])
    return gain


def gaussian(stream_key, shape, width, most, split=(), kind=jnp.bfloat16):
    entries = width * jax.random.normal(stream_key, shape, jnp.float32)
    if split:
        entries = entries * block_scale(stream_key, shape, split, -0.22, 0.18)
    return jnp.clip(entries, -most, most).astype(kind)


def setup_inputs(seed: int = 0) -> dict:
    key_of = jax.random.split(jax.random.key(seed), 19)
    return {
        "tokens": gaussian(key_of[0], (TOKENS, D), 1.0, 6.0, ((0, 32),)),
        "latents": gaussian(key_of[1], (LATS, D), 1.0, 6.0, ((0, 32),)),
        "valid_mask": draw_valid_mask(jax.random.fold_in(key_of[18], 71), 0),
        "out_cotangent": gaussian(key_of[3], (TOKENS, D), 1.0, 6.0, ((0, 32),)),
        "latent_cotangent": gaussian(key_of[4], (LATS, D), 1.0, 6.0, ((0, 32),)),
        "norm_gains": jnp.clip(1.0 + 0.1 * jax.random.normal(key_of[5], (8, D), jnp.float32), 0.5, 1.5).astype(jnp.bfloat16),
        "local_qkv": gaussian(key_of[6], (3 * D, D), D ** -0.5, 0.21875, ((0, 32),)),
        "local_out": gaussian(key_of[7], (D, D), (D // 16) ** -0.5, 0.875, ((0, 32),)),
        "token_up": gaussian(key_of[8], (FF, D), D ** -0.5, 0.21875, ((0, 32),)),
        "token_down": gaussian(key_of[9], (D, FF), FF ** -0.5, 0.109375, ((0, 32),)),
        "read_qkv": gaussian(key_of[10], (3 * D, D), D ** -0.5, 0.21875, ((0, 32),)),
        "read_out": gaussian(key_of[11], (D, D), (D // 16) ** -0.5, 0.875, ((0, 32),)),
        "global_qkv": gaussian(key_of[12], (3 * D, D), D ** -0.5, 0.21875, ((0, 32),)),
        "global_out": gaussian(key_of[13], (D, D), (D // 8) ** -0.5, 0.625, ((0, 32),)),
        "latent_up": gaussian(key_of[14], (FF, D), D ** -0.5, 0.21875, ((0, 32),)),
        "latent_down": gaussian(key_of[15], (D, FF), FF ** -0.5, 0.109375, ((0, 32),)),
        "write_qkv": gaussian(key_of[16], (3 * D, D), D ** -0.5, 0.21875, ((0, 32),)),
        "write_out": gaussian(key_of[17], (D, D), (D // 2) ** -0.5, 0.3125, ((0, 32),)),
    }


@jax.custom_vjp
def low(v):
    return lax.optimization_barrier(v.astype(jnp.bfloat16)).astype(jnp.float32)

@jax.custom_vjp
def low_back(v):
    return v

def low_keep(v):
    return (low(v), None)

def low_pass(kept, grad):
    return (grad,)

def back_keep(v):
    return (v, None)

def back_low(kept, grad):
    return (low(grad),)
low.defvjp(low_keep, low_pass)
low_back.defvjp(back_keep, back_low)
norm_eps = 1e-05
mask_fill = -1000000000.0

def apply_weight(row_block, weight):
    return jnp.einsum('...i,oi->...o', row_block, weight, precision=lax.Precision.HIGHEST)

def layer_norm(values, gain_row):
    centered = values - lax.optimization_barrier(jnp.mean(values, axis=-1, keepdims=True))
    variance = lax.optimization_barrier(jnp.mean(centered * centered, axis=-1, keepdims=True))
    return centered * lax.rsqrt(variance + norm_eps) * gain_row

def split_heads(values):
    return values.reshape(values.shape[:-1] + (values.shape[-1] // HDIM, HDIM))

def attention(query_norm, key_norm, qkv_weight, out_weight, key_bias):
    model_width = query_norm.shape[-1]
    query_rows = low(low_back(apply_weight(query_norm, qkv_weight[:model_width])))
    key_rows = low(low_back(apply_weight(key_norm, qkv_weight[model_width:2 * model_width])))
    value_rows = low(low_back(apply_weight(key_norm, qkv_weight[2 * model_width:])))
    raw_scores = jnp.einsum('bqhe,bkhe->bhqk', split_heads(query_rows), split_heads(key_rows), precision=lax.Precision.HIGHEST) * HDIM ** (-0.5)
    scores = low_back(raw_scores) + key_bias[:, None, :, :]
    row_max = lax.optimization_barrier(jnp.max(scores, axis=-1, keepdims=True))
    exponent = jnp.exp(scores - row_max)
    probs = low(exponent / lax.optimization_barrier(jnp.sum(exponent, axis=-1, keepdims=True)))
    mixed = jnp.einsum('bhqk,bkhe->bqhe', probs, split_heads(value_rows), precision=lax.Precision.HIGHEST)
    mixed = low(low_back(mixed.reshape(query_rows.shape)))
    return low_back(apply_weight(mixed, out_weight))

def feed_forward(norm_rows, up_weight, down_weight):
    hidden_pre = low_back(apply_weight(norm_rows, up_weight))
    activated = low(jax.nn.gelu(hidden_pre, approximate=True))
    return low_back(apply_weight(activated, down_weight))

def image_layer(residual, latent, valid_row, gain_all, weight_all):
    group_count = SLOTS // GROUP
    residual_in = residual.reshape(group_count, GROUP, D)
    token_bias = jnp.where(valid_row > 0.5, 0.0, mask_fill).reshape(group_count, 1, GROUP)
    local_norm = low(layer_norm(residual_in, gain_all[0]))
    residual_one = residual_in + attention(local_norm, local_norm, weight_all[0], weight_all[1], token_bias)
    token_norm = low(layer_norm(residual_one, gain_all[1]))
    residual_two = residual_one + feed_forward(token_norm, weight_all[2], weight_all[3])
    latent_in = latent.reshape(group_count, LAT, D)
    read_query = low(layer_norm(latent_in, gain_all[2]))
    read_keys = low(layer_norm(residual_two, gain_all[3]))
    latent_one = latent_in + attention(read_query, read_keys, weight_all[4], weight_all[5], token_bias)
    latent_one = latent_one.reshape(1, group_count * LAT, D)
    global_norm = low(layer_norm(latent_one, gain_all[4]))
    latent_two = latent_one + attention(global_norm, global_norm, weight_all[6], weight_all[7], jnp.zeros((1, 1, group_count * LAT), jnp.float32))
    latent_norm = low(layer_norm(latent_two, gain_all[5]))
    latent_out = latent_two + feed_forward(latent_norm, weight_all[8], weight_all[9])
    latent_groups = latent_out.reshape(group_count, LAT, D)
    write_query = low(layer_norm(residual_two, gain_all[6]))
    write_keys = low(layer_norm(latent_groups, gain_all[7]))
    residual_out = residual_two + attention(write_query, write_keys, weight_all[10], weight_all[11], jnp.zeros((group_count, 1, LAT), jnp.float32))
    masked = residual_out * valid_row.reshape(group_count, GROUP, 1)
    return (masked.reshape(SLOTS, D), latent_out.reshape(group_count * LAT, D))

def reference(tokens, latents, valid_mask, out_cotangent, latent_cotangent, norm_gains, local_qkv, local_out, token_up, token_down, read_qkv, read_out, global_qkv, global_out, latent_up, latent_down, write_qkv, write_out):
    weight_all = tuple((matrix.astype(jnp.float32) for matrix in (local_qkv, local_out, token_up, token_down, read_qkv, read_out, global_qkv, global_out, latent_up, latent_down, write_qkv, write_out)))
    gain_all = norm_gains.astype(jnp.float32)
    images = TOKENS // SLOTS
    per_image = SLOTS // GROUP * LAT
    residuals = tokens.astype(jnp.float32).reshape(images, SLOTS, D)
    latent_rows = latents.astype(jnp.float32).reshape(images, per_image, D)
    valid_rows = valid_mask.astype(jnp.float32).reshape(images, SLOTS)
    grad_out_rows = out_cotangent.astype(jnp.float32).reshape(images, SLOTS, D)
    grad_lat_rows = latent_cotangent.astype(jnp.float32).reshape(images, per_image, D)

    def image_step(summed, slices):
        residual, latent, valid_row, grad_out, grad_lat = slices

        def layer_of(residual_in, latent_in, gains_in, weights_in):
            return image_layer(residual_in, latent_in, valid_row, gains_in, weights_in)
        results, pullback = jax.vjp(layer_of, residual, latent, gain_all, weight_all)
        grad_residual, grad_latent, grad_gain, grad_weights = pullback((grad_out, grad_lat))
        summed = jax.tree.map(jnp.add, summed, (grad_gain, grad_weights))
        return (summed, (results[0], results[1], grad_residual, grad_latent))
    start = jax.tree.map(jnp.zeros_like, (gain_all, weight_all))
    summed, stacked = lax.scan(image_step, start, (residuals, latent_rows, valid_rows, grad_out_rows, grad_lat_rows))
    grad_gain, grad_weights = summed
    return (stacked[0].reshape(TOKENS, D).astype(jnp.bfloat16), stacked[1].reshape(LATS, D).astype(jnp.bfloat16), stacked[2].reshape(TOKENS, D), stacked[3].reshape(LATS, D), grad_gain, grad_weights[0], grad_weights[1], grad_weights[2], grad_weights[3], grad_weights[4], grad_weights[5], grad_weights[6], grad_weights[7], grad_weights[8], grad_weights[9], grad_weights[10], grad_weights[11])
```

```python
import functools
import jax
import jax.numpy as jnp
from jax import lax
from jax.experimental import pallas as pl
from jax.experimental.pallas import tpu as pltpu
from jax.sharding import PartitionSpec as P

HDIM = 64
GROUP = 256
LAT = 8
SLOTS = 4096


norm_eps = 1e-05
mask_fill = -1000000000.0


def project(row_block, weight):
    return lax.dot_general(
        row_block,
        weight,
        (((row_block.ndim - 1,), (1,)), ((), ())),
        preferred_element_type=jnp.float32,
    )


def back_project(grad_rows, weight):
    return lax.dot_general(
        grad_rows,
        weight,
        (((grad_rows.ndim - 1,), (0,)), ((), ())),
        preferred_element_type=jnp.float32,
    )


def weight_grad(grad_rows, in_rows):
    grad_flat = grad_rows.reshape(-1, grad_rows.shape[-1])
    in_flat = in_rows.reshape(-1, in_rows.shape[-1])
    return lax.dot_general(
        grad_flat, in_flat, (((0,), (0,)), ((), ())), preferred_element_type=jnp.float32
    )


def layer_norm(values, gain_row):
    centered = values - jnp.mean(values, axis=-1, keepdims=True)
    variance = jnp.mean(centered * centered, axis=-1, keepdims=True)
    return centered * lax.rsqrt(variance + norm_eps) * gain_row


def norm_back(values, gain_row, grad_rows):
    normed, pullback = jax.vjp(layer_norm, values, gain_row)
    return pullback(grad_rows)


def gelu_tanh(values):
    return jax.nn.gelu(values, approximate=True)


def split_heads(values):
    return values.reshape(values.shape[:-1] + (values.shape[-1] // HDIM, HDIM))


def scores_of(query_bf, key_bf, key_bias):
    raw_scores = jnp.einsum(
        "bqhe,bkhe->bhqk",
        split_heads(query_bf),
        split_heads(key_bf),
        preferred_element_type=jnp.float32,
    )
    return raw_scores * HDIM ** (-0.5) + key_bias[:, None, :, :]


def attend(query_bf, key_bf, value_bf, key_bias):
    scores = scores_of(query_bf, key_bf, key_bias)
    row_max = jnp.max(scores, axis=-1, keepdims=True)
    exponent = jnp.exp(scores - row_max)
    row_sum = jnp.sum(exponent, axis=-1, keepdims=True)
    probs_low = (exponent / row_sum).astype(jnp.bfloat16)
    mixed = jnp.einsum(
        "bhqk,bkhe->bqhe", probs_low, split_heads(value_bf), preferred_element_type=jnp.float32
    )
    return (mixed.reshape(query_bf.shape).astype(jnp.bfloat16), row_max + jnp.log(row_sum))


def attend_back(query_bf, key_bf, value_bf, key_bias, log_total, grad_mixed):
    scores = scores_of(query_bf, key_bf, key_bias)
    probs_full = jnp.exp(scores - log_total)
    probs_low = probs_full.astype(jnp.bfloat16)
    value_heads = split_heads(value_bf)
    grad_heads = split_heads(grad_mixed)
    grad_probs = jnp.einsum(
        "bqhe,bkhe->bhqk", grad_heads, value_heads, preferred_element_type=jnp.float32
    )
    grad_scores = probs_full * (
        grad_probs - jnp.sum(grad_probs * probs_full, axis=-1, keepdims=True)
    )
    grad_scores = grad_scores.astype(jnp.bfloat16)
    score_scale = HDIM ** (-0.5)
    grad_query = (
        jnp.einsum(
            "bhqk,bkhe->bqhe", grad_scores, split_heads(key_bf), preferred_element_type=jnp.float32
        )
        * score_scale
    )
    grad_key = (
        jnp.einsum(
            "bhqk,bqhe->bkhe",
            grad_scores,
            split_heads(query_bf),
            preferred_element_type=jnp.float32,
        )
        * score_scale
    )
    grad_value = jnp.einsum(
        "bhqk,bqhe->bkhe", probs_low, grad_heads, preferred_element_type=jnp.float32
    )
    return (
        grad_query.reshape(query_bf.shape),
        grad_key.reshape(key_bf.shape),
        grad_value.reshape(value_bf.shape),
    )


def queries_keys(query_norm, key_norm, qkv_weight):
    model_width = query_norm.shape[-1]
    query_bf = project(query_norm, qkv_weight[:model_width]).astype(jnp.bfloat16)
    key_values = project(key_norm, qkv_weight[model_width:]).astype(jnp.bfloat16)
    return (query_bf, key_values)


def block_attention(query_norm, key_norm, qkv_weight, out_weight, key_bias):
    model_width = query_norm.shape[-1]
    query_bf, key_values = queries_keys(query_norm, key_norm, qkv_weight)
    mixed, log_total = attend(
        query_bf, key_values[..., :model_width], key_values[..., model_width:], key_bias
    )
    return (project(mixed, out_weight), (query_bf, key_values, mixed, log_total))


def block_attention_back(
    query_norm, key_norm, qkv_weight, out_weight, key_bias, kept, grad_branch
):
    model_width = query_norm.shape[-1]
    query_bf, key_values, mixed, log_total = kept
    branch_bf = grad_branch.astype(jnp.bfloat16)
    grad_mixed = back_project(branch_bf, out_weight).astype(jnp.bfloat16)
    grad_query, grad_key, grad_value = attend_back(
        query_bf,
        key_values[..., :model_width],
        key_values[..., model_width:],
        key_bias,
        log_total,
        grad_mixed,
    )
    query_grad_bf = grad_query.astype(jnp.bfloat16)
    keyval_grad_bf = jnp.concatenate([grad_key, grad_value], axis=-1).astype(jnp.bfloat16)
    grad_qkv = jnp.concatenate(
        [weight_grad(query_grad_bf, query_norm), weight_grad(keyval_grad_bf, key_norm)], axis=0
    )
    grad_out = weight_grad(branch_bf, mixed)
    grad_query_norm = back_project(query_grad_bf, qkv_weight[:model_width])
    grad_key_norm = back_project(keyval_grad_bf, qkv_weight[model_width:])
    return (grad_query_norm, grad_key_norm, grad_qkv, grad_out)


def mlp_forward(norm_rows, up_weight, down_weight):
    hidden_pre = project(norm_rows, up_weight)
    activated = gelu_tanh(hidden_pre).astype(jnp.bfloat16)
    return (project(activated, down_weight), activated)


def mlp_back(norm_rows, up_weight, down_weight, act_bf, grad_branch):
    hidden_pre = project(norm_rows, up_weight)
    _, pullback = jax.vjp(gelu_tanh, hidden_pre)
    branch_bf = grad_branch.astype(jnp.bfloat16)
    grad_act = back_project(branch_bf, down_weight)
    grad_pre = pullback(grad_act)[0].astype(jnp.bfloat16)
    model_width = branch_bf.shape[-1]
    pieces = act_bf.shape[-1] // model_width
    return (
        back_project(grad_pre, up_weight),
        weight_grad(grad_pre, norm_rows),
        [
            weight_grad(branch_bf, act_bf[..., model_width * j : model_width * (j + 1)])
            for j in range(pieces)
        ],
    )


MESH_ID = pl.DeviceIdType.MESH
ALL_AXES = ("dp", "fsdp")


def place():
    dp_index = lax.axis_index("dp")
    fsdp_index = lax.axis_index("fsdp")
    return (dp_index // 2, dp_index % 2, fsdp_index // 2, fsdp_index % 2)


def device(z, core, y, x):
    return {"dp": z * 2 + core, "fsdp": y * 2 + x}


def remote(src, dst, send_sem, recv_sem, target):
    return pltpu.make_async_remote_copy(
        src, dst, send_sem, recv_sem, device_id=target, device_id_type=MESH_ID
    )


def greet(peers):
    barrier = pltpu.get_barrier_semaphore()
    for peer in peers:
        pl.semaphore_signal(barrier, inc=1, device_id=peer, device_id_type=MESH_ID)
    pl.semaphore_wait(barrier, len(peers))


def scatter_kernel(groups, count, *refs):
    chunks = len(groups)
    ins = refs[:count]
    outs = refs[count : count + chunks]
    own, pair, first_b, first_c, second_b, second_c, last = refs[count + chunks : count + chunks + 7]
    local_sem, s0, q0, s1, q1, s2, q2, s3, q3 = refs[count + chunks + 7 :]
    z, core, y, x = place()
    half = ins[0].shape[-1] // 2
    sibling = device(z, 1 - core, y, x)
    over_x = device(z, core, y, 1 - x)
    over_y = device(z, core, 1 - y, x)
    over_z = [device((z + step) % 4, core, y, x) for step in (1, 2, 3)]
    greet([sibling, over_x, over_y] + over_z)
    f32 = jnp.float32
    bf16 = jnp.bfloat16
    left = pl.ds(0, half)
    right = pl.ds(half, half)
    rows_of = [sum(rows for _, rows in group) for group in groups]

    def copies_pair(k):
        made = []
        offset = 0
        for j, (i, rows) in enumerate(groups[k]):
            spot = pl.ds(offset, rows)
            made.append(
                (
                    pltpu.make_async_copy(
                        ins[i].at[:, core], own.at[k, :, :, :, spot, :], local_sem.at[k, j]
                    ),
                    remote(
                        ins[i].at[:, 1 - core],
                        pair.at[k, :, :, :, spot, :],
                        s0.at[k, j],
                        q0.at[k, j],
                        sibling,
                    ),
                )
            )
            offset += rows
        return made

    def copies_first(k):
        spot = pl.ds(0, rows_of[k])
        return [
            remote(
                own.at[k, :, 1 - y, :, spot, left],
                first_b.at[k, :, :, spot],
                s1.at[k, 0],
                q1.at[k, 0],
                over_y,
            ),
            remote(
                own.at[k, :, :, 1 - x, spot, right],
                first_c.at[k, :, :, spot],
                s1.at[k, 1],
                q1.at[k, 1],
                over_x,
            ),
        ]

    def copies_second(k):
        spot = pl.ds(0, rows_of[k])
        return [
            remote(
                first_b.at[k, :, 1 - x, spot],
                second_b.at[k, :, spot],
                s2.at[k, 0],
                q2.at[k, 0],
                over_x,
            ),
            remote(
                first_c.at[k, :, 1 - y, spot],
                second_c.at[k, :, spot],
                s2.at[k, 1],
                q2.at[k, 1],
                over_y,
            ),
        ]

    def copies_last(k):
        spot = pl.ds(0, rows_of[k])
        made = []
        for step in (1, 2, 3):
            goal = (z + step) % 4
            for side, (source, place_at) in enumerate(((second_b, left), (second_c, right))):
                made.append(
                    remote(
                        source.at[k, goal, spot],
                        last.at[k, step - 1, spot, place_at],
                        s3.at[k, step - 1, side],
                        q3.at[k, step - 1, side],
                        over_z[step - 1],
                    )
                )
        return made

    pairs = [copies_pair(k) for k in range(chunks)]
    firsts = [copies_first(k) for k in range(chunks)]
    seconds = [copies_second(k) for k in range(chunks)]
    lasts = [copies_last(k) for k in range(chunks)]

    def start_pair(k):
        for local, far in pairs[k]:
            local.start()
            far.start()

    def stage_pair(k):
        rows = rows_of[k]
        for local, far in pairs[k]:
            local.wait()
            far.wait_recv()
        if k + 2 < chunks:
            start_pair(k + 2)

        def step(i, carry):
            zz, yy, xx = i // 4, (i // 2) % 2, i % 2
            own[k, zz, yy, xx, :rows] = (
                own[k, zz, yy, xx, :rows].astype(f32) + pair[k, zz, yy, xx, :rows].astype(f32)
            ).astype(bf16)
            return carry

        lax.fori_loop(0, 16, step, 0)
        for copy in firsts[k]:
            copy.start()

    def stage_first(k):
        rows = rows_of[k]
        for copy in firsts[k]:
            copy.wait_recv()

        def step(i, carry):
            zz, other = i // 2, i % 2
            first_b[k, zz, other, :rows] = (
                own[k, zz, y, other, :rows, :half].astype(f32)
                + first_b[k, zz, other, :rows].astype(f32)
            ).astype(bf16)
            first_c[k, zz, other, :rows] = (
                own[k, zz, other, x, :rows, half:].astype(f32)
                + first_c[k, zz, other, :rows].astype(f32)
            ).astype(bf16)
            return carry

        lax.fori_loop(0, 8, step, 0)
        for copy in seconds[k]:
            copy.start()

    def stage_second(k):
        rows = rows_of[k]
        for copy in seconds[k]:
            copy.wait_recv()

        def step(zz, carry):
            second_b[k, zz, :rows] = (
                first_b[k, zz, x, :rows].astype(f32) + second_b[k, zz, :rows].astype(f32)
            ).astype(bf16)
            second_c[k, zz, :rows] = (
                first_c[k, zz, y, :rows].astype(f32) + second_c[k, zz, :rows].astype(f32)
            ).astype(bf16)
            return carry

        lax.fori_loop(0, 4, step, 0)
        for copy in lasts[k]:
            copy.start()

    def stage_last(k):
        rows = rows_of[k]
        for copy in lasts[k]:
            copy.wait_recv()
        for source, low in ((second_b, 0), (second_c, half)):
            total = source[k, z, :rows].astype(f32)
            for step in range(3):
                total = total + last[k, step, :rows, low : low + half].astype(f32)
            outs[k][:, low : low + half] = total

    start_pair(0)
    if chunks > 1:
        start_pair(1)
    for turn in range(chunks + 3):
        if turn < chunks:
            stage_pair(turn)
        if 0 <= turn - 1 < chunks:
            stage_first(turn - 1)
        if 0 <= turn - 2 < chunks:
            stage_second(turn - 2)
        if 0 <= turn - 3 < chunks:
            stage_last(turn - 3)
    for k in range(chunks):
        for _, far in pairs[k]:
            far.wait_send()
        for copy in firsts[k] + seconds[k] + lasts[k]:
            copy.wait_send()


def scatter_sums(arrays, groups, call_id):
    cols = arrays[0].shape[1]
    half = cols // 2
    chunks = len(groups)
    rows_of = [sum(rows for _, rows in group) for group in groups]
    most = max(rows_of)
    parts = max(len(group) for group in groups)
    ins = [array.reshape(4, 2, 2, 2, array.shape[0] // 32, cols) for array in arrays]
    bf16 = jnp.bfloat16
    vmem = pltpu.VMEM
    dma = pltpu.SemaphoreType.DMA
    return pl.pallas_call(
        functools.partial(scatter_kernel, groups, len(ins)),
        out_shape=[jax.ShapeDtypeStruct((rows, cols), jnp.float32) for rows in rows_of],
        in_specs=[pl.BlockSpec(memory_space=pl.ANY)] * len(ins),
        out_specs=[pl.BlockSpec(memory_space=pltpu.VMEM)] * chunks,
        scratch_shapes=[
            vmem((chunks, 4, 2, 2, most, cols), bf16),
            vmem((chunks, 4, 2, 2, most, cols), bf16),
            vmem((chunks, 4, 2, most, half), bf16),
            vmem((chunks, 4, 2, most, half), bf16),
            vmem((chunks, 4, most, half), bf16),
            vmem((chunks, 4, most, half), bf16),
            vmem((chunks, 3, most, cols), bf16),
            dma((chunks, parts)),
            dma((chunks, parts)),
            dma((chunks, parts)),
            dma((chunks, 2)),
            dma((chunks, 2)),
            dma((chunks, 2)),
            dma((chunks, 2)),
            dma((chunks, 3, 2)),
            dma((chunks, 3, 2)),
        ],
        compiler_params=pltpu.CompilerParams(
            collective_id=call_id, has_side_effects=True, vmem_limit_bytes=66 * 1024 * 1024
        ),
        name="scatter_sums",
    )(*ins)


def fold_columns(shard):
    rows, cols = shard.shape
    width = 768 if cols % 768 == 0 else cols
    return shard.reshape(rows, cols // width, width).transpose(1, 0, 2).reshape(-1, width)


def unfold_columns(folded, devices):
    width = folded.shape[1]
    rows = width // devices
    pieces = folded.shape[0] // width
    split = folded.reshape(devices, pieces, rows, width).transpose(0, 2, 1, 3)
    return split.reshape(width, pieces * width)


def gather_packed(shards_in, devices):
    packed = jnp.concatenate(shards_in, axis=0)
    gathered = lax.all_gather(packed, ALL_AXES, axis=0)
    found = []
    offset = 0
    for shard in shards_in:
        rows = shard.shape[0]
        found.append(gathered[:, offset : offset + rows].reshape(devices * rows, shard.shape[1]))
        offset += rows
    return found


def reduce_grads(groups, devices):
    arrays = []
    chunks = []
    for group in groups:
        chunk = []
        for array in group:
            chunk.append((len(arrays), array.shape[0] // devices))
            arrays.append(array.astype(jnp.bfloat16))
        chunks.append(chunk)
    if (lax.axis_size("dp"), lax.axis_size("fsdp")) == (8, 4):
        sums = scatter_sums(arrays, chunks, 1)
        found = []
        for total, chunk in zip(sums, chunks):
            offset = 0
            parts = []
            for _, rows in chunk:
                parts.append(total[offset : offset + rows])
                offset += rows
            found.append(parts)
        return found
    return [
        [
            lax.psum_scatter(array.astype(jnp.float32), ALL_AXES, scatter_dimension=0, tiled=True)
            for array in group
        ]
        for group in groups
    ]


def shards(
    tokens,
    latents,
    valid_mask,
    out_cotangent,
    latent_cotangent,
    norm_gains,
    local_qkv,
    local_out,
    token_up,
    token_down,
    read_qkv,
    read_out,
    global_qkv,
    global_out,
    latent_up,
    latent_down,
    write_qkv,
    write_out,
):
    model_width = tokens.shape[1]
    group_count = tokens.shape[0] // GROUP
    latent_count = group_count * LAT
    per_image = SLOTS // GROUP
    valid_rows = valid_mask.astype(jnp.float32)
    token_bias = (
        jnp.where(valid_mask > 0, 0.0, mask_fill).astype(jnp.float32).reshape(group_count, 1, GROUP)
    )
    local_image = (
        lax.axis_index("fsdp") * group_count + jnp.arange(latent_count, dtype=jnp.int32) // LAT
    ) // per_image
    remote_image = jnp.arange(lax.axis_size("fsdp") * latent_count, dtype=jnp.int32) // (
        LAT * per_image
    )
    latent_bias = jnp.where(local_image[:, None] == remote_image[None, :], 0.0, mask_fill).astype(
        jnp.float32
    )[None]
    empty_bias = jnp.zeros((group_count, 1, LAT), jnp.float32)
    devices = lax.axis_size("dp") * lax.axis_size("fsdp")
    gain_part = norm_gains.reshape(1, -1)
    gain_part = jnp.pad(gain_part, ((0, 7), (0, model_width - gain_part.shape[1])))
    weights = gather_packed(
        [local_qkv, local_out, token_up, fold_columns(token_down), gain_part], devices
    )
    token_side = (weights[0], weights[1], weights[2], unfold_columns(weights[3], devices))
    gain_all = weights[4].reshape(devices, 8, model_width)[:, 0, : norm_gains.size]
    gain_all = gain_all.reshape(devices, 8, norm_gains.shape[1]).transpose(1, 0, 2)
    gain_rows = gain_all.reshape(8, model_width).astype(jnp.float32)
    weights = gather_packed(
        [
            read_qkv,
            read_out,
            global_qkv,
            global_out,
            latent_up,
            fold_columns(latent_down),
            write_qkv,
            write_out,
        ],
        devices,
    )
    latent_side = tuple(weights[:5]) + (unfold_columns(weights[5], devices),) + tuple(weights[6:])
    residual_in = tokens.astype(jnp.float32).reshape(group_count, GROUP, model_width)
    local_norm = layer_norm(residual_in, gain_rows[0]).astype(jnp.bfloat16)
    branch, local_kept = block_attention(
        local_norm, local_norm, token_side[0], token_side[1], token_bias
    )
    residual_one = residual_in + branch
    token_norm = layer_norm(residual_one, gain_rows[1]).astype(jnp.bfloat16)
    branch, token_act = mlp_forward(token_norm, token_side[2], token_side[3])
    residual_two = residual_one + branch
    latent_in = latents.astype(jnp.float32).reshape(group_count, LAT, model_width)
    read_query = layer_norm(latent_in, gain_rows[2]).astype(jnp.bfloat16)
    read_keys = layer_norm(residual_two, gain_rows[3]).astype(jnp.bfloat16)
    branch, read_kept = block_attention(
        read_query, read_keys, latent_side[0], latent_side[1], token_bias
    )
    latent_one = (latent_in + branch).reshape(latent_count, model_width)
    global_norm = layer_norm(latent_one, gain_rows[4]).astype(jnp.bfloat16)
    global_query, global_keyval = queries_keys(global_norm, global_norm, latent_side[2])
    gathered = lax.all_gather(global_keyval, "fsdp", axis=0, tiled=True)
    global_mixed, global_total = attend(
        global_query[None],
        gathered[None, :, :model_width],
        gathered[None, :, model_width:],
        latent_bias,
    )
    latent_two = latent_one + project(global_mixed[0], latent_side[3])
    latent_norm = layer_norm(latent_two, gain_rows[5]).astype(jnp.bfloat16)
    branch, latent_act = mlp_forward(latent_norm, latent_side[4], latent_side[5])
    latent_out = latent_two + branch
    latent_groups = latent_out.reshape(group_count, LAT, model_width)
    write_query = layer_norm(residual_two, gain_rows[6]).astype(jnp.bfloat16)
    write_keys = layer_norm(latent_groups, gain_rows[7]).astype(jnp.bfloat16)
    branch, write_kept = block_attention(
        write_query, write_keys, latent_side[6], latent_side[7], empty_bias
    )
    residual_out = residual_two + branch
    mask_rows = valid_rows.reshape(group_count, GROUP, 1)
    out_tokens = (residual_out * mask_rows).reshape(-1, model_width).astype(jnp.bfloat16)
    out_latents = latent_out.astype(jnp.bfloat16)
    back_all = (token_side[0], token_side[1], token_side[2], token_side[3]) + tuple(latent_side)
    grad_residual_out = (
        out_cotangent.astype(jnp.float32).reshape(group_count, GROUP, model_width) * mask_rows
    )
    grad_latent_out = latent_cotangent.astype(jnp.float32)
    grad_query_norm, grad_key_norm, write_qkv_grad, write_out_grad = block_attention_back(
        write_query,
        write_keys,
        back_all[10],
        back_all[11],
        empty_bias,
        write_kept,
        grad_residual_out,
    )
    grad_values, grad_gain_six = norm_back(residual_two, gain_rows[6], grad_query_norm)
    grad_residual_two = grad_residual_out + grad_values
    grad_values, grad_gain_seven = norm_back(latent_groups, gain_rows[7], grad_key_norm)
    grad_latent_out = grad_latent_out + grad_values.reshape(latent_count, model_width)
    grad_norm_rows, latent_up_grad, latent_down_grad = mlp_back(
        latent_norm, back_all[8], back_all[9], latent_act, grad_latent_out
    )
    grad_values, grad_gain_five = norm_back(latent_two, gain_rows[5], grad_norm_rows)
    grad_latent_two = grad_latent_out + grad_values
    branch_bf = grad_latent_two.astype(jnp.bfloat16)
    grad_mixed = back_project(branch_bf, back_all[7]).astype(jnp.bfloat16)
    grad_query, grad_key, grad_value = attend_back(
        global_query[None],
        gathered[None, :, :model_width],
        gathered[None, :, model_width:],
        latent_bias,
        global_total,
        grad_mixed[None],
    )
    own_both = lax.psum_scatter(
        jnp.concatenate([grad_key[0], grad_value[0]], axis=-1).astype(jnp.bfloat16),
        "fsdp",
        scatter_dimension=0,
        tiled=True,
    )
    query_grad_bf = grad_query[0].astype(jnp.bfloat16)
    keyval_grad_bf = own_both.astype(jnp.bfloat16)
    global_qkv_grad = jnp.concatenate(
        [weight_grad(query_grad_bf, global_norm), weight_grad(keyval_grad_bf, global_norm)], axis=0
    )
    global_out_grad = weight_grad(branch_bf, global_mixed[0])
    grad_norm_rows = back_project(query_grad_bf, back_all[6][:model_width]) + back_project(
        keyval_grad_bf, back_all[6][model_width:]
    )
    grad_values, grad_gain_four = norm_back(latent_one, gain_rows[4], grad_norm_rows)
    grad_latent_one = (grad_latent_two + grad_values).reshape(group_count, LAT, model_width)
    grad_query_norm, grad_key_norm, read_qkv_grad, read_out_grad = block_attention_back(
        read_query, read_keys, back_all[4], back_all[5], token_bias, read_kept, grad_latent_one
    )
    grad_values, grad_gain_two = norm_back(latent_in, gain_rows[2], grad_query_norm)
    grad_latent_in = grad_latent_one + grad_values
    grad_values, grad_gain_three = norm_back(residual_two, gain_rows[3], grad_key_norm)
    grad_residual_two = grad_residual_two + grad_values
    grad_norm_rows, token_up_grad, token_down_grad = mlp_back(
        token_norm, back_all[2], back_all[3], token_act, grad_residual_two
    )
    grad_values, grad_gain_one = norm_back(residual_one, gain_rows[1], grad_norm_rows)
    grad_residual_one = grad_residual_two + grad_values
    grad_query_norm, grad_key_norm, local_qkv_grad, local_out_grad = block_attention_back(
        local_norm, local_norm, back_all[0], back_all[1], token_bias, local_kept, grad_residual_one
    )
    grad_values, grad_gain_zero = norm_back(
        residual_in, gain_rows[0], grad_query_norm + grad_key_norm
    )
    grad_residual_in = grad_residual_one + grad_values
    gain_grads = jnp.stack(
        [
            grad_gain_zero,
            grad_gain_one,
            grad_gain_two,
            grad_gain_three,
            grad_gain_four,
            grad_gain_five,
            grad_gain_six,
            grad_gain_seven,
        ]
    )
    gain_cols = norm_gains.shape[1]
    gain_split = gain_grads.reshape(8, devices, gain_cols).transpose(1, 0, 2)
    gain_split = gain_split.reshape(devices, 1, 8 * gain_cols)
    gain_split = jnp.pad(gain_split, ((0, 0), (0, 7), (0, model_width - 8 * gain_cols)))
    sums = reduce_grads(
        [
            [write_qkv_grad, write_out_grad],
            [latent_up_grad],
            latent_down_grad,
            [global_qkv_grad, global_out_grad],
            [read_qkv_grad, read_out_grad],
            [token_up_grad],
            token_down_grad,
            [local_qkv_grad, local_out_grad, gain_split.reshape(-1, model_width)],
        ],
        devices,
    )
    gain_sum = sums[7][2][0, : 8 * gain_cols].reshape(8, gain_cols)
    return (
        out_tokens,
        out_latents,
        grad_residual_in.reshape(-1, model_width),
        grad_latent_in.reshape(-1, model_width),
        gain_sum,
        sums[7][0],
        sums[7][1],
        sums[5][0],
        jnp.concatenate(sums[6], axis=1),
        sums[4][0],
        sums[4][1],
        sums[3][0],
        sums[3][1],
        sums[1][0],
        jnp.concatenate(sums[2], axis=1),
        sums[0][0],
        sums[0][1],
    )


def solution(mesh):
    in_specs = (
        P(("dp", "fsdp"), None),
        P(("dp", "fsdp"), None),
        P(("dp", "fsdp")),
        P(("dp", "fsdp"), None),
        P(("dp", "fsdp"), None),
        P(None, ("dp", "fsdp")),
        P(("dp", "fsdp"), None),
        P(("dp", "fsdp"), None),
        P(("dp", "fsdp"), None),
        P(("dp", "fsdp"), None),
        P(("dp", "fsdp"), None),
        P(("dp", "fsdp"), None),
        P(("dp", "fsdp"), None),
        P(("dp", "fsdp"), None),
        P(("dp", "fsdp"), None),
        P(("dp", "fsdp"), None),
        P(("dp", "fsdp"), None),
        P(("dp", "fsdp"), None),
    )
    out_specs = (
        P(("dp", "fsdp"), None),
        P(("dp", "fsdp"), None),
        P(("dp", "fsdp"), None),
        P(("dp", "fsdp"), None),
        P(None, ("dp", "fsdp")),
        P(("dp", "fsdp"), None),
        P(("dp", "fsdp"), None),
        P(("dp", "fsdp"), None),
        P(("dp", "fsdp"), None),
        P(("dp", "fsdp"), None),
        P(("dp", "fsdp"), None),
        P(("dp", "fsdp"), None),
        P(("dp", "fsdp"), None),
        P(("dp", "fsdp"), None),
        P(("dp", "fsdp"), None),
        P(("dp", "fsdp"), None),
        P(("dp", "fsdp"), None),
    )
    return jax.shard_map(shards, mesh=mesh, in_specs=in_specs, out_specs=out_specs, check_vma=False)
```
